32 devices in a mesh: groups: 2 (over x), gx: 4 (over y, core), gy: 4 (over z).
Axes of the slice: x: 2, y: 2, z: 4, core: 2. Of those that a mesh axis runs over, the one named last changes fastest.
Arguments:
- tokens: bfloat16 [64, 2, 16384], P('groups', None, 'gx'), parts along dimension 0
- norm_gain: bfloat16 [16384], P('gx'), may hold values from 0.099609375 to 1.8984375
- qkv_weight: bfloat16 [16384, 8, 18, 128], P('gx', 'gy'), may hold values from -0.046875 to 0.046875
- out_weight: bfloat16 [128, 128, 16384], P('gy', None, 'gx'), may hold values from -0.125 to 0.125
- kv_cache: bfloat16 [64, 384, 2, 8, 128], P(('groups', 'gx', 'gy')), parts along dimension 0
- lengths: int32 [64], P(('groups', 'gx', 'gy')), parts along dimension 0, may hold values from 1 to 384, as said below
- positions: int32 [64], P('groups'), parts along dimension 0, may hold values from 0 to 4095
Outputs:
- layer_out: float32 [64, 2, 16384], P(('groups', 'gy'), None, 'gx'), parts along dimension 0
The draws below stay inside these ranges and needn't reach their ends.
There are 2 independent parts, one for each index of `groups`. The reference program is written for one: setup_inputs(seed, part) draws one part's arguments, and reference() takes and returns one part's arrays. A program takes and returns all parts, laid end to end along the dimension named above; an argument that names none is the same for every part. Nothing has to cross between parts.
Inputs may be any that keep to these rules, and one draw needn't show every extreme that they name: Cache slots 0 to lengths - 1 of a row hold its earlier tokens; some row has exactly 384.
All inputs are finite; a program needn't handle non-finite values.
Results may differ from the reference program's by a relative error of at most 0.025.
Values may be sent and summed in bfloat16 or wider, within the bound.
A program may use at most 192 MiB of HBM per device.

```python
import math
import jax
import jax.numpy as jnp
from jax import lax

D = 16384
HQ = 128
KV = 8
HD = 128
GQ = 16
MAXLEN = 384
ROWS = 32


def draw_tokens(key, part):
    key_base = jax.random.fold_in(key, 11)
    noise_key, scale_key = jax.random.split(key_base)
    columns = jnp.arange(D, dtype=jnp.float32) / D
    noise_part = jax.random.normal(noise_key, (ROWS, 2, D), jnp.float32)
    column_scale = jnp.exp(columns * jnp.log(10.0)) / 3.2
    row_scale = jnp.exp(jax.random.uniform(scale_key, (ROWS, 2, 1), jnp.float32, -0.7, 0.7))
    return (noise_part * column_scale * row_scale).astype(jnp.bfloat16)


def draw_kv_cache(key, part):
    key_base = jax.random.fold_in(key, 23)
    value_key = jax.random.fold_in(key_base, 0)
    entries = jax.random.normal(value_key, (ROWS, MAXLEN, 2, KV, HD), jnp.float32)
    return entries.astype(jnp.bfloat16)


def draw_lengths(key, part):
    key_base = jax.random.fold_in(key, 37)
    long_key, short_key, pick_key, top_key = jax.random.split(key_base, 4)
    long_draw = jax.random.randint(long_key, (ROWS,), 1, MAXLEN + 1)
    short_draw = jax.random.randint(short_key, (ROWS,), 1, MAXLEN // 16 + 2)
    picker = jax.random.randint(pick_key, (ROWS,), 0, 4)
    chosen = jnp.where(picker == 0, short_draw, long_draw)
    top_row = jax.random.randint(top_key, (), 0, ROWS)
    chosen = jnp.where(jnp.arange(ROWS, dtype=jnp.int32) == top_row, MAXLEN, chosen)
    return chosen.astype(jnp.int32)


def place_ends(drawn, stream_key, low, largest):
    longest = drawn.shape.index(max(drawn.shape))
    spots = []
    for shift in (0, 1):
        where = [jax.random.randint(jax.random.fold_in(stream_key, axis), (), 0, length) for axis, length in enumerate(drawn.shape)]
        where[longest] = (where[longest] + shift) % drawn.shape[longest]
        spots.append(tuple(where))
    return drawn.at[spots[0]].set(low).at[spots[1]].set(largest)


def levels(stream_key, dims, pieces, smallest, top_value):
    def one(axis_at, blocks):
        steps = jax.random.uniform(jax.random.fold_in(jax.random.fold_in(stream_key, 6), axis_at), (blocks,), jnp.float32, smallest / len(pieces), top_value / len(pieces))
        return jnp.repeat(jnp.exp(steps), dims[axis_at] // blocks).reshape((-1,) + (1,) * (len(dims) - axis_at - 1))

    level = one(*pieces[0])
    for cut in pieces[1:]:
        level = level * one(*cut)
    return level


def bell_draw(stream_key, dims, scale, most, cuts=(), kind=jnp.bfloat16):
    loudness = levels(stream_key, dims, cuts, -0.22, 0.18) if cuts else 1.0
    array = jax.random.normal(stream_key, dims, jnp.float32) * scale * loudness
    return jnp.minimum(jnp.maximum(array, -most), most).astype(kind)


def setup_inputs(seed: int = 0, part: int = 0) -> dict:
    key_of = jax.random.split(jax.random.key(seed), 8)
    part_keys = jax.random.split(jax.random.fold_in(key_of[7], part), 8)
    tokens = draw_tokens(jax.random.fold_in(jax.random.fold_in(key_of[7], part), 71), part)
    norm_gain = jnp.clip(1.0 + 0.18 * jax.random.normal(key_of[1], (D,), jnp.float32), 0.099609375, 1.8984375).astype(jnp.bfloat16)
    qkv_weight = bell_draw(key_of[2], (D, KV, GQ + 2, HD), D ** -0.5, 0.046875, ((0, 4), (1, 4)))
    out_weight = bell_draw(key_of[3], (HQ, HD, D), (GQ * HD) ** -0.5, 0.125, ((0, 4), (2, 4)))
    kv_cache = draw_kv_cache(jax.random.fold_in(jax.random.fold_in(key_of[7], part), 71), part)
    lengths = draw_lengths(jax.random.fold_in(jax.random.fold_in(key_of[7], part), 71), part)
    positions = place_ends(jax.random.randint(part_keys[6], (ROWS,), 0, 4096), jax.random.fold_in(part_keys[6], 1), 0, 4095).astype(jnp.int32)
    return dict(tokens=tokens, norm_gain=norm_gain, qkv_weight=qkv_weight, out_weight=out_weight, kv_cache=kv_cache, lengths=lengths, positions=positions)


norm_eps = 1e-05
rope_base = 500000.0

def rotate(values, places):
    half_dim = values.shape[-1] // 2
    index_half = jnp.arange(half_dim, dtype=jnp.float32)
    frequency = rope_base ** (-2.0 * index_half / values.shape[-1])
    angles = places[..., None] * frequency
    cosine = jnp.cos(angles)
    sine_part = jnp.sin(angles)
    front_half = values[..., :half_dim]
    back_half = values[..., half_dim:]
    return jnp.concatenate([front_half * cosine - back_half * sine_part, back_half * cosine + front_half * sine_part], axis=-1)

def attend(queries, key_new, value_new, cache_rows, length):
    scale_factor = 1.0 / math.sqrt(queries.shape[-1])
    query_wide = queries.astype(jnp.float32)
    old_keys = cache_rows[:, :, 0].astype(jnp.float32)
    old_values = cache_rows[:, :, 1].astype(jnp.float32)
    scores_old = jnp.einsum('rtgid,rsgd->rtgis', query_wide, old_keys) * scale_factor
    slot_ids = jnp.arange(cache_rows.shape[1], dtype=jnp.int32)
    visible = slot_ids[None, :] < length[:, None]
    scores_old = jnp.where(visible[:, None, None, None, :], scores_old, -1e+30)
    scores_new = jnp.einsum('rtgid,rugd->rtgiu', query_wide, key_new.astype(jnp.float32)) * scale_factor
    token_ids = jnp.arange(queries.shape[1], dtype=jnp.int32)
    causal = token_ids[:, None] >= token_ids[None, :]
    scores_new = jnp.where(causal[None, :, None, None, :], scores_new, -1e+30)
    highest = jnp.maximum(lax.optimization_barrier(jnp.max(scores_old, axis=-1)), lax.optimization_barrier(jnp.max(scores_new, axis=-1)))
    expo_old = jnp.exp(scores_old - highest[..., None])
    expo_new = jnp.exp(scores_new - highest[..., None])
    denominator = lax.optimization_barrier(jnp.sum(expo_old, axis=-1)) + lax.optimization_barrier(jnp.sum(expo_new, axis=-1))
    weight_old = (expo_old / denominator[..., None]).astype(jnp.bfloat16)
    weight_new = (expo_new / denominator[..., None]).astype(jnp.bfloat16)
    attended = jnp.einsum('rtgis,rsgd->rtgid', weight_old.astype(jnp.float32), old_values)
    attended = attended + jnp.einsum('rtgiu,rugd->rtgid', weight_new.astype(jnp.float32), value_new.astype(jnp.float32))
    return attended.astype(jnp.bfloat16)

def reference(tokens, norm_gain, qkv_weight, out_weight, kv_cache, lengths, positions):
    tokens_wide = tokens.astype(jnp.float32)
    hidden = (tokens_wide * norm_gain.astype(jnp.float32)).astype(jnp.bfloat16)
    inv_rms = lax.rsqrt(lax.optimization_barrier(jnp.sum(tokens_wide * tokens_wide, axis=-1)) / D + norm_eps)
    projected = jnp.dot(hidden.reshape(ROWS * 2, D), qkv_weight.reshape(D, KV * (GQ + 2) * HD), preferred_element_type=jnp.float32)
    projected = projected.reshape(ROWS, 2, KV, GQ + 2, HD) * inv_rms[:, :, None, None, None]
    places = (positions[:, None] + jnp.arange(2, dtype=jnp.int32)[None, :]).astype(jnp.float32)
    queries = rotate(projected[:, :, :, :GQ], places[:, :, None, None]).astype(jnp.bfloat16)
    key_new = rotate(projected[:, :, :, GQ], places[:, :, None]).astype(jnp.bfloat16)
    value_new = projected[:, :, :, GQ + 1].astype(jnp.bfloat16)

    def one_row(packed):
        return attend(packed[0], packed[1], packed[2], packed[3], packed[4])
    attended = lax.map(one_row, (queries[:, None], key_new[:, None], value_new[:, None], kv_cache[:, None], lengths[:, None]))
    attended = attended.reshape(ROWS * 2, HQ * HD)
    update = jnp.dot(attended, out_weight.reshape(HQ * HD, D), preferred_element_type=jnp.float32)
    return tokens_wide + update.reshape(ROWS, 2, D)
```

```python
import functools
import math

import jax
import jax.numpy as jnp
from jax import lax
from jax.experimental import pallas as pl
from jax.experimental.pallas import tpu as pltpu
from jax.sharding import PartitionSpec as P

D = 16384


norm_eps = 1e-05
rope_base = 500000.0


def rotate(values, places):
    half_dim = values.shape[-1] // 2
    index_half = jnp.arange(half_dim, dtype=jnp.float32)
    frequency = rope_base ** (-2.0 * index_half / values.shape[-1])
    angles = places[..., None] * frequency
    cosine = jnp.cos(angles)
    sine_part = jnp.sin(angles)
    front_half = values[..., :half_dim]
    back_half = values[..., half_dim:]
    return jnp.concatenate(
        [front_half * cosine - back_half * sine_part, back_half * cosine + front_half * sine_part],
        axis=-1,
    )


def finish(projected, positions, first_row, row_count):
    group_size = projected.shape[3] - 2
    placed = lax.dynamic_slice_in_dim(positions, first_row, row_count, 0)
    places = (placed[:, None] + jnp.arange(2, dtype=jnp.int32)[None, :]).astype(jnp.float32)
    queries = rotate(projected[:, :, :, :group_size], places[:, :, None, None])
    key_new = rotate(projected[:, :, :, group_size : group_size + 1], places[:, :, None, None])
    value_new = projected[:, :, :, group_size + 1 :]
    return jnp.concatenate([queries, key_new, value_new], axis=3).astype(jnp.bfloat16)


def attend(queries, key_new, value_new, cache_rows, length):
    scale_factor = 1.0 / math.sqrt(queries.shape[-1])
    scores_old = (
        jnp.einsum(
            "rtgid,rsgd->rtgis", queries, cache_rows[:, :, 0], preferred_element_type=jnp.float32
        )
        * scale_factor
    )
    slot_ids = jnp.arange(cache_rows.shape[1], dtype=jnp.int32)
    visible = slot_ids[None, :] < length[:, None]
    scores_old = jnp.where(visible[:, None, None, None, :], scores_old, -1e30)
    scores_new = (
        jnp.einsum("rtgid,rugd->rtgiu", queries, key_new, preferred_element_type=jnp.float32)
        * scale_factor
    )
    token_ids = jnp.arange(queries.shape[1], dtype=jnp.int32)
    causal = token_ids[:, None] >= token_ids[None, :]
    scores_new = jnp.where(causal[None, :, None, None, :], scores_new, -1e30)
    highest = jnp.maximum(jnp.max(scores_old, axis=-1), jnp.max(scores_new, axis=-1))
    expo_old = jnp.exp(scores_old - highest[..., None])
    expo_new = jnp.exp(scores_new - highest[..., None])
    denominator = jnp.sum(expo_old, axis=-1) + jnp.sum(expo_new, axis=-1)
    weight_old = (expo_old / denominator[..., None]).astype(jnp.bfloat16)
    weight_new = (expo_new / denominator[..., None]).astype(jnp.bfloat16)
    attended = jnp.einsum(
        "rtgis,rsgd->rtgid", weight_old, cache_rows[:, :, 1], preferred_element_type=jnp.float32
    )
    attended = attended + jnp.einsum(
        "rtgiu,rugd->rtgid", weight_new, value_new, preferred_element_type=jnp.float32
    )
    return attended.astype(jnp.bfloat16)


def project_kernel(
    places, block_rows, steps, depth, tokens_ref, gain_ref, weight_ref, out_ref, held, total, squares, sems
):
    groups, columns, head_dim = 2, weight_ref.shape[1], weight_ref.shape[3]
    slots = held.shape[0]
    total_tokens = tokens_ref.shape[0]

    def fetch(step, slot, column):
        start = step * depth
        if not isinstance(step, int):
            start = pl.multiple_of(start, depth)
        return pltpu.make_async_copy(
            weight_ref.at[pl.ds(start, depth), column], held.at[slot, column], sems.at[slot, column]
        )

    for step in range(slots - 1):
        for column in range(columns):
            fetch(step, step, column).start()
    total[...] = jnp.zeros_like(total)
    squares[...] = jnp.zeros_like(squares)
    feature = lax.broadcasted_iota(jnp.int32, (128, 256), 0)
    target = lax.broadcasted_iota(jnp.int32, (128, 256), 1)
    spreads = [
        jnp.where(target == feature * groups + group, 1.0, 0.0).astype(jnp.bfloat16)
        for group in range(groups)
    ]

    @pl.loop(0, steps)
    def _(step):
        slot = lax.rem(step, slots)

        @pl.when(step + slots - 1 < steps)
        def _():
            later = step + slots - 1
            for column in range(columns):
                fetch(later, lax.rem(later, slots), column).start()

        start = pl.multiple_of(step * depth, depth)
        wide = tokens_ref[:, pl.ds(start, depth)].astype(jnp.float32)
        squares[...] += sum(
            wide[:, at : at + 128] * wide[:, at : at + 128] for at in range(0, depth, 128)
        )
        hidden = (wide * gain_ref[:, pl.ds(start, depth)].astype(jnp.float32)).astype(jnp.bfloat16)
        parts = []
        for at in range(0, depth, 128):
            spread = [
                jnp.dot(
                    hidden[:, at : at + 128], spreads[group], preferred_element_type=jnp.float32
                ).astype(jnp.bfloat16)
                for group in range(groups)
            ]
            parts.append(
                jnp.concatenate(
                    [
                        spread[group][row : row + block_rows]
                        for row in range(0, total_tokens, block_rows)
                        for group in range(groups)
                    ],
                    axis=0,
                )
            )
        left = jnp.concatenate(parts, axis=1)
        for column in range(0, columns, 2):
            for near in (column, column + 1):
                fetch(step, slot, near).wait()
            right = jnp.concatenate(
                [
                    held.at[slot, near].reshape(depth * groups, head_dim)[...]
                    for near in (column, column + 1)
                ],
                axis=1,
            )
            span = pl.ds(column * head_dim, 2 * head_dim)
            total[:, span] += jnp.dot(left, right, preferred_element_type=jnp.float32)

    width = columns * head_dim
    out_ref[:, :width] = total[...].astype(jnp.bfloat16)
    summed = jnp.sum(squares[...], axis=1, keepdims=True)
    coarse = summed.astype(jnp.bfloat16).astype(jnp.float32)
    lane = lax.broadcasted_iota(jnp.int32, (total_tokens, 128), 1)
    extra = jnp.where(lane < 64, coarse, summed - coarse)
    extra = jnp.concatenate(
        [
            extra[row : row + block_rows]
            for row in range(0, total_tokens, block_rows)
            for _ in range(groups)
        ],
        axis=0,
    )
    out_ref[:, width:] = extra.astype(jnp.bfloat16)


def project(tokens, norm_gain, qkv_weight, places):
    total_rows, pair, local_width = tokens.shape
    groups, columns, head_dim = qkv_weight.shape[1:]
    total_tokens = total_rows * pair
    block_rows = total_tokens // places
    depth, slots = 512, 3
    steps = local_width // depth
    view = jnp.transpose(qkv_weight, (0, 2, 1, 3))
    vmem = pl.BlockSpec(memory_space=pltpu.VMEM)
    return pl.pallas_call(
        functools.partial(project_kernel, places, block_rows, steps, depth),
        out_shape=jax.ShapeDtypeStruct(
            (total_tokens * groups, (columns + 1) * head_dim), jnp.bfloat16
        ),
        in_specs=[vmem, vmem, pl.BlockSpec(memory_space=pl.ANY)],
        out_specs=vmem,
        scratch_shapes=[
            pltpu.VMEM((slots, columns, depth, groups, head_dim), jnp.bfloat16),
            pltpu.VMEM((total_tokens * groups, columns * head_dim), jnp.float32),
            pltpu.VMEM((total_tokens, 128), jnp.float32),
            pltpu.SemaphoreType.DMA((slots, columns)),
        ],
        compiler_params=pltpu.CompilerParams(vmem_limit_bytes=40 << 20),
    )(tokens.reshape(total_tokens, local_width), norm_gain.reshape(1, local_width), view)


def body(tokens, norm_gain, qkv_weight, out_weight, kv_cache, lengths, positions):
    rows_local = kv_cache.shape[0]
    head_devices = lax.axis_size("gy")
    width_index = lax.axis_index("gx")
    head_index = lax.axis_index("gy")
    total_rows = tokens.shape[0]
    local_width = tokens.shape[2]
    groups_local = qkv_weight.shape[1]
    group_width = qkv_weight.shape[2]
    head_dim = qkv_weight.shape[3]
    group_size = group_width - 2
    block_rows = rows_local * head_devices
    places = lax.axis_size("gx")
    if groups_local == 2 and group_width % 2 == 0 and local_width % 512 == 0:
        partial_value = project(tokens, norm_gain, qkv_weight, places)
        partial_value = partial_value.reshape(places, groups_local * block_rows * 2, -1)
        pieces = lax.all_to_all(partial_value, "gx", split_axis=0, concat_axis=0)
        summed = jnp.sum(pieces.astype(jnp.float32), axis=0)
        summed = summed.reshape(groups_local, block_rows, 2, group_width + 1, head_dim)
        block_squares = summed[0, :, :, group_width, 0] + summed[0, :, :, group_width, 64]
        block_sum = jnp.transpose(summed[:, :, :, :group_width], (1, 2, 0, 3, 4))
    else:
        tokens_wide = tokens.astype(jnp.float32)
        hidden = (tokens_wide * norm_gain.astype(jnp.float32)).astype(jnp.bfloat16)
        squares = jnp.sum(tokens_wide * tokens_wide, axis=-1)
        partial_value = jnp.dot(
            hidden.reshape(total_rows * 2, local_width),
            qkv_weight.reshape(local_width, -1),
            preferred_element_type=jnp.float32,
        )
        partial_value = partial_value.reshape(total_rows, 2, groups_local, group_width, head_dim)
        block_sum, block_squares = (
            lax.psum_scatter(partial_value, "gx", scatter_dimension=0, tiled=True),
            lax.psum_scatter(squares, "gx", scatter_dimension=0, tiled=True),
        )
    inv_rms = lax.rsqrt(block_squares / D + norm_eps)
    ready = finish(
        block_sum * inv_rms[:, :, None, None, None], positions, width_index * block_rows, block_rows
    )
    packed = lax.all_to_all(ready, "gy", split_axis=0, concat_axis=2, tiled=True)
    queries = packed[:, :, :, :group_size]
    key_new = packed[:, :, :, group_size]
    value_new = packed[:, :, :, group_size + 1]
    attended = attend(queries, key_new, value_new, kv_cache, lengths)
    regrouped = lax.all_to_all(attended, "gy", split_axis=2, concat_axis=0, tiled=True)
    out_flat = out_weight.reshape(-1, local_width)
    row_piece = lax.all_gather(regrouped, "gx", axis=0, tiled=True)
    piece_rows = row_piece.shape[0]
    product = jnp.dot(
        row_piece.reshape(piece_rows * 2, -1), out_flat, preferred_element_type=jnp.float32
    )
    terms = product.astype(jnp.bfloat16).reshape(head_devices, -1, 2, local_width)
    arrived = lax.all_to_all(terms, "gy", split_axis=0, concat_axis=0)
    own_sum = jnp.sum(arrived.astype(jnp.float32), axis=0)
    row_share = total_rows // head_devices
    residual = lax.dynamic_slice_in_dim(tokens, head_index * row_share, row_share, 0).astype(
        jnp.float32
    )
    return residual + own_sum


def solution(mesh):
    return jax.shard_map(
        body,
        mesh=mesh,
        in_specs=(
            P("groups", None, "gx"),
            P("gx"),
            P("gx", "gy", None, None),
            P("gy", None, "gx"),
            P(("groups", "gx", "gy"), None, None, None, None),
            P(("groups", "gx", "gy")),
            P("groups"),
        ),
        out_specs=P(("groups", "gy"), None, "gx"),
        check_vma=False,
    )
```

```python
import functools
import math

import jax
import jax.numpy as jnp
from jax import lax
from jax.experimental import pallas as pl
from jax.experimental.pallas import tpu as pltpu
from jax.sharding import PartitionSpec as P

D = 16384


norm_eps = 1e-05
rope_base = 500000.0


def rotate(values, places):
    half_dim = values.shape[-1] // 2
    index_half = jnp.arange(half_dim, dtype=jnp.float32)
    frequency = rope_base ** (-2.0 * index_half / values.shape[-1])
    angles = places[..., None] * frequency
    cosine = jnp.cos(angles)
    sine_part = jnp.sin(angles)
    front_half = values[..., :half_dim]
    back_half = values[..., half_dim:]
    return jnp.concatenate(
        [front_half * cosine - back_half * sine_part, back_half * cosine + front_half * sine_part],
        axis=-1,
    )


def finish(projected, positions, first_row, row_count):
    group_size = projected.shape[3] - 2
    placed = lax.dynamic_slice_in_dim(positions, first_row, row_count, 0)
    places = (placed[:, None] + jnp.arange(2, dtype=jnp.int32)[None, :]).astype(jnp.float32)
    queries = rotate(projected[:, :, :, :group_size], places[:, :, None, None])
    key_new = rotate(projected[:, :, :, group_size : group_size + 1], places[:, :, None, None])
    value_new = projected[:, :, :, group_size + 1 :]
    return jnp.concatenate([queries, key_new, value_new], axis=3).astype(jnp.bfloat16)


def attend(queries, key_new, value_new, cache_rows, length):
    scale_factor = 1.0 / math.sqrt(queries.shape[-1])
    scores_old = (
        jnp.einsum(
            "rtgid,rsgd->rtgis", queries, cache_rows[:, :, 0], preferred_element_type=jnp.float32
        )
        * scale_factor
    )
    slot_ids = jnp.arange(cache_rows.shape[1], dtype=jnp.int32)
    visible = slot_ids[None, :] < length[:, None]
    scores_old = jnp.where(visible[:, None, None, None, :], scores_old, -1e30)
    scores_new = (
        jnp.einsum("rtgid,rugd->rtgiu", queries, key_new, preferred_element_type=jnp.float32)
        * scale_factor
    )
    token_ids = jnp.arange(queries.shape[1], dtype=jnp.int32)
    causal = token_ids[:, None] >= token_ids[None, :]
    scores_new = jnp.where(causal[None, :, None, None, :], scores_new, -1e30)
    highest = jnp.maximum(jnp.max(scores_old, axis=-1), jnp.max(scores_new, axis=-1))
    expo_old = jnp.exp(scores_old - highest[..., None])
    expo_new = jnp.exp(scores_new - highest[..., None])
    denominator = jnp.sum(expo_old, axis=-1) + jnp.sum(expo_new, axis=-1)
    weight_old = (expo_old / denominator[..., None]).astype(jnp.bfloat16)
    weight_new = (expo_new / denominator[..., None]).astype(jnp.bfloat16)
    attended = jnp.einsum(
        "rtgis,rsgd->rtgid", weight_old, cache_rows[:, :, 1], preferred_element_type=jnp.float32
    )
    attended = attended + jnp.einsum(
        "rtgiu,rugd->rtgid", weight_new, value_new, preferred_element_type=jnp.float32
    )
    return attended.astype(jnp.bfloat16)


def bring(weight_ref, chunk_ref, sems, first):
    copies = [
        pltpu.make_async_copy(weight_ref.at[:, first + at], chunk_ref.at[at], sems.at[at])
        for at in range(chunk_ref.shape[0])
    ]
    for copy in copies:
        copy.start()
    return copies


def open_kernel(block_rows, depth, tokens_ref, gain_ref, weight_ref, left_ref, extra_ref, chunk_ref, sems):
    groups = 2
    total_tokens, local_width = tokens_ref.shape
    copies = bring(weight_ref, chunk_ref, sems, 0)
    feature = lax.broadcasted_iota(jnp.int32, (128, 256), 0)
    target = lax.broadcasted_iota(jnp.int32, (128, 256), 1)
    spreads = [
        jnp.where(target == feature * groups + group, 1.0, 0.0).astype(jnp.bfloat16)
        for group in range(groups)
    ]

    def order(pieces):
        return jnp.concatenate(
            [
                pieces[group][row : row + block_rows]
                for row in range(0, total_tokens, block_rows)
                for group in range(groups)
            ],
            axis=0,
        )

    def step(at, squares):
        start = pl.multiple_of(at * depth, depth)
        wide = tokens_ref[:, pl.ds(start, depth)].astype(jnp.float32)
        hidden = (wide * gain_ref[:, pl.ds(start, depth)].astype(jnp.float32)).astype(jnp.bfloat16)
        for near in range(0, depth, 128):
            squares += wide[:, near : near + 128] * wide[:, near : near + 128]
            spread = [
                jnp.dot(
                    hidden[:, near : near + 128], spreads[group], preferred_element_type=jnp.float32
                ).astype(jnp.bfloat16)
                for group in range(groups)
            ]
            begin = pl.multiple_of((start + near) * groups, 256)
            left_ref[:, pl.ds(begin, 256)] = order(spread)
        return squares

    squares = lax.fori_loop(
        0, local_width // depth, step, jnp.zeros((total_tokens, 128), jnp.float32)
    )
    summed = jnp.sum(squares, axis=1, keepdims=True)
    coarse = summed.astype(jnp.bfloat16).astype(jnp.float32)
    lane = lax.broadcasted_iota(jnp.int32, (total_tokens, 128), 1)
    extra = jnp.where(lane < 64, coarse, summed - coarse)
    extra_ref[...] = order([extra, extra]).astype(jnp.bfloat16)
    for copy in copies:
        copy.wait()


def multiply_kernel(following, left_ref, chunk_ref, weight_ref, out_ref, *rest):
    copies = []
    if following is not None:
        next_ref, total, sems = rest
        copies = bring(weight_ref, next_ref, sems, following)
    else:
        (total,) = rest
    count, contraction, head_dim = chunk_ref.shape
    total[...] = jnp.zeros_like(total)

    @pl.loop(0, contraction // 1024)
    def _(step):
        span = pl.ds(pl.multiple_of(step * 1024, 1024), 1024)
        left = left_ref[:, span]
        for column in range(0, count, 2):
            right = jnp.concatenate([chunk_ref[column, span], chunk_ref[column + 1, span]], axis=1)
            total[:, column * head_dim : (column + 2) * head_dim] += jnp.dot(
                left, right, preferred_element_type=jnp.float32
            )

    out_ref[...] = total[...].astype(jnp.bfloat16)
    for copy in copies:
        copy.wait()


def project(tokens, norm_gain, qkv_weight, places):
    total_rows, pair, local_width = tokens.shape
    groups, columns, head_dim = qkv_weight.shape[1:]
    total_tokens = total_rows * pair
    count = columns // 3
    view = jnp.transpose(qkv_weight, (0, 2, 1, 3))
    vmem = pl.BlockSpec(memory_space=pltpu.VMEM)
    hbm = pl.BlockSpec(memory_space=pl.ANY)
    chunk_shape = jax.ShapeDtypeStruct((count, local_width, groups, head_dim), jnp.bfloat16)
    rows = total_tokens * groups
    params = pltpu.CompilerParams(vmem_limit_bytes=14 << 20)
    left, extra, chunk = pl.pallas_call(
        functools.partial(open_kernel, total_tokens // places, 512),
        out_shape=(
            jax.ShapeDtypeStruct((rows, local_width * groups), jnp.bfloat16),
            jax.ShapeDtypeStruct((rows, head_dim), jnp.bfloat16),
            chunk_shape,
        ),
        in_specs=[vmem, vmem, hbm],
        out_specs=(vmem, vmem, vmem),
        scratch_shapes=[pltpu.SemaphoreType.DMA((count,))],
        compiler_params=params,
    )(tokens.reshape(total_tokens, local_width), norm_gain.reshape(1, local_width), view)
    results = []
    for following in (count, 2 * count, None):
        last = following is None
        out_shape = [jax.ShapeDtypeStruct((rows, count * head_dim), jnp.bfloat16)]
        scratch = [pltpu.VMEM((rows, count * head_dim), jnp.float32)]
        if not last:
            out_shape.append(chunk_shape)
            scratch.append(pltpu.SemaphoreType.DMA((count,)))
        flat = chunk.reshape(count, local_width * groups, head_dim)
        got = pl.pallas_call(
            functools.partial(multiply_kernel, following),
            out_shape=out_shape,
            in_specs=[vmem, vmem, hbm],
            out_specs=[vmem] * len(out_shape),
            scratch_shapes=scratch,
            compiler_params=params,
        )(left, flat, view)
        results.append(got[0])
        if not last:
            chunk = got[1]
    return jnp.concatenate(results + [extra], axis=1)


def body(tokens, norm_gain, qkv_weight, out_weight, kv_cache, lengths, positions):
    rows_local = kv_cache.shape[0]
    head_devices = lax.axis_size("gy")
    width_index = lax.axis_index("gx")
    head_index = lax.axis_index("gy")
    total_rows = tokens.shape[0]
    local_width = tokens.shape[2]
    groups_local = qkv_weight.shape[1]
    group_width = qkv_weight.shape[2]
    head_dim = qkv_weight.shape[3]
    group_size = group_width - 2
    block_rows = rows_local * head_devices
    places = lax.axis_size("gx")
    if groups_local == 2 and group_width % 6 == 0 and local_width % 512 == 0:
        partial_value = project(tokens, norm_gain, qkv_weight, places)
        partial_value = partial_value.reshape(places, groups_local * block_rows * 2, -1)
        pieces = lax.all_to_all(partial_value, "gx", split_axis=0, concat_axis=0)
        summed = jnp.sum(pieces.astype(jnp.float32), axis=0)
        summed = summed.reshape(groups_local, block_rows, 2, group_width + 1, head_dim)
        block_squares = summed[0, :, :, group_width, 0] + summed[0, :, :, group_width, 64]
        block_sum = jnp.transpose(summed[:, :, :, :group_width], (1, 2, 0, 3, 4))
    else:
        tokens_wide = tokens.astype(jnp.float32)
        hidden = (tokens_wide * norm_gain.astype(jnp.float32)).astype(jnp.bfloat16)
        squares = jnp.sum(tokens_wide * tokens_wide, axis=-1)
        partial_value = jnp.dot(
            hidden.reshape(total_rows * 2, local_width),
            qkv_weight.reshape(local_width, -1),
            preferred_element_type=jnp.float32,
        )
        partial_value = partial_value.reshape(total_rows, 2, groups_local, group_width, head_dim)
        block_sum, block_squares = (
            lax.psum_scatter(partial_value, "gx", scatter_dimension=0, tiled=True),
            lax.psum_scatter(squares, "gx", scatter_dimension=0, tiled=True),
        )
    inv_rms = lax.rsqrt(block_squares / D + norm_eps)
    ready = finish(
        block_sum * inv_rms[:, :, None, None, None], positions, width_index * block_rows, block_rows
    )
    packed = lax.all_to_all(ready, "gy", split_axis=0, concat_axis=2, tiled=True)
    queries = packed[:, :, :, :group_size]
    key_new = packed[:, :, :, group_size]
    value_new = packed[:, :, :, group_size + 1]
    attended = attend(queries, key_new, value_new, kv_cache, lengths)
    regrouped = lax.all_to_all(attended, "gy", split_axis=2, concat_axis=0, tiled=True)
    out_flat = out_weight.reshape(-1, local_width)
    row_piece = lax.all_gather(regrouped, "gx", axis=0, tiled=True)
    piece_rows = row_piece.shape[0]
    product = jnp.dot(
        row_piece.reshape(piece_rows * 2, -1), out_flat, preferred_element_type=jnp.float32
    )
    terms = product.astype(jnp.bfloat16).reshape(head_devices, -1, 2, local_width)
    arrived = lax.all_to_all(terms, "gy", split_axis=0, concat_axis=0)
    own_sum = jnp.sum(arrived.astype(jnp.float32), axis=0)
    row_share = total_rows // head_devices
    residual = lax.dynamic_slice_in_dim(tokens, head_index * row_share, row_share, 0).astype(
        jnp.float32
    )
    return residual + own_sum


def solution(mesh):
    return jax.shard_map(
        body,
        mesh=mesh,
        in_specs=(
            P("groups", None, "gx"),
            P("gx"),
            P("gx", "gy", None, None),
            P("gy", None, "gx"),
            P(("groups", "gx", "gy"), None, None, None, None),
            P(("groups", "gx", "gy")),
            P("groups"),
        ),
        out_specs=P(("groups", "gy"), None, "gx"),
        check_vma=False,
    )
```
